32 devices in a mesh: grp: 2 (over x), ctx: 4 (over y, core), head: 4 (over z).
Axes of the slice: x: 2, y: 2, z: 4, core: 2. Of those that a mesh axis runs over, the one named last changes fastest.
Arguments:
- queries: bfloat16 [8192, 4096], P(('grp', 'ctx'), 'head'), parts along dimension 0, may hold values from -6 to 6
- keys: bfloat16 [8192, 4096], P(('grp', 'ctx'), 'head'), parts along dimension 0, may hold values from -6 to 6
- values: bfloat16 [8192, 4096], P(('grp', 'ctx'), 'head'), parts along dimension 0, may hold values from -6 to 6
- init_state: float32 [64, 128, 128], P(('grp', 'head')), parts along dimension 0, may hold values from -192 to 192
- out_grad: bfloat16 [8192, 4096], P(('grp', 'ctx'), 'head'), parts along dimension 0, may hold values from -6 to 6
Outputs:
- output: bfloat16 [8192, 4096], P(('grp', 'ctx'), 'head'), parts along dimension 0
- query_grad: bfloat16 [8192, 4096], P(('grp', 'ctx'), 'head'), parts along dimension 0
- key_grad: bfloat16 [8192, 4096], P(('grp', 'ctx'), 'head'), parts along dimension 0
- value_grad: bfloat16 [8192, 4096], P(('grp', 'ctx'), 'head'), parts along dimension 0
- state_grad: float32 [64, 128, 128], P(('grp', 'head')), parts along dimension 0
The draws below stay inside these ranges and needn't reach their ends.
There are 2 independent parts, one for each index of `grp`. The reference program is written for one: setup_inputs(seed, part) draws one part's arguments, and reference() takes and returns one part's arrays. A program takes and returns all parts, laid end to end along the dimension named above; each array names one. Nothing has to cross between parts.
All inputs are finite; a program needn't handle non-finite values.
Results may differ from the reference program's by a relative error of at most 0.0058.
Values sent between devices are 32-bit elements; how exact they have to be, the bound alone decides.
A program may use at most 128 MiB of HBM per device.

```python
import jax
import jax.numpy as jnp
from jax import lax

HEADS = 32
HEAD_DIM = 128
TOK_DEV = 1024
WIDTH = 4096
TOKENS = 4096


def steps_of(own_key, extent, shards, low, largest):
    def one(axis_at, blocks):
        heights = jax.random.uniform(jax.random.fold_in(jax.random.fold_in(own_key, 6), axis_at), (blocks,), jnp.float32, low / len(shards), largest / len(shards))
        return jnp.repeat(jnp.exp(heights), extent[axis_at] // blocks).reshape((-1,) + (1,) * (len(extent) - axis_at - 1))

    level = one(*shards[0])
    for cut in shards[1:]:
        level = level * one(*cut)
    return level


def centred(key, shape, scale, reach, shards=(), kind=jnp.bfloat16):
    level = steps_of(key, shape, shards, -0.22, 0.18) if shards else 1.0
    drawn = jax.random.normal(key, shape, jnp.float32) * scale * level
    return jnp.minimum(jnp.maximum(drawn, -reach), reach).astype(kind)


def setup_inputs(seed: int = 0, part: int = 0) -> dict:
    key_of = jax.random.split(jax.random.key(seed), 6)
    own_keys = jax.random.split(jax.random.fold_in(key_of[5], part), 6)
    return {
        "queries": centred(own_keys[0], (TOKENS, WIDTH), 1.0, 6.0, ((0, 4), (1, 4))),
        "keys": centred(own_keys[1], (TOKENS, WIDTH), 1.0, 6.0, ((0, 4), (1, 4))),
        "values": centred(own_keys[2], (TOKENS, WIDTH), 1.0, 6.0, ((0, 4), (1, 4))),
        "init_state": centred(own_keys[3], (HEADS, HEAD_DIM, HEAD_DIM), (max(1, TOK_DEV // 32)), 192.0, ((0, 4),), jnp.float32),
        "out_grad": centred(own_keys[4], (TOKENS, WIDTH), 1.0, 6.0, ((0, 4), (1, 4))),
    }


def round_half(x):
    return lax.optimization_barrier(x.astype(jnp.bfloat16)).astype(jnp.float32)

def reference(queries, keys, values, init_state, out_grad):
    blocks = queries.shape[0] // TOK_DEV
    shape = (blocks, TOK_DEV, HEADS, HEAD_DIM)
    q_all = queries.astype(jnp.float32).reshape(shape)
    k_all = keys.astype(jnp.float32).reshape(shape)
    v_all = values.astype(jnp.float32).reshape(shape)
    g_all = out_grad.astype(jnp.float32).reshape(shape)
    causal = jnp.arange(TOK_DEV)[:, None] >= jnp.arange(TOK_DEV)[None, :]
    block_state = jnp.einsum('cthd,cthe->chde', k_all, v_all)
    zero_state = jnp.zeros((1, HEADS, HEAD_DIM, HEAD_DIM), jnp.float32)
    earlier = jnp.concatenate([zero_state, jnp.cumsum(block_state, axis=0)[:-1]], axis=0)
    prefix_b = round_half(init_state[None] + earlier)

    def forward_block(items):
        q_blk, k_blk, v_blk, p_blk, g_blk = items
        raw = jnp.einsum('thd,shd->hts', q_blk, k_blk)
        scores = round_half(jnp.where(causal[None], raw, 0.0))
        attended = jnp.einsum('thd,hde->the', q_blk, p_blk) + jnp.einsum('hts,she->the', scores, v_blk)
        inv_rms = lax.rsqrt(lax.optimization_barrier(jnp.mean(attended * attended, axis=-1, keepdims=True)) + 1e-06)
        normed = attended * inv_rms
        grad_att = round_half(inv_rms * (g_blk - normed * lax.optimization_barrier(jnp.mean(g_blk * normed, axis=-1, keepdims=True))))
        block_grad = jnp.einsum('thd,the->hde', q_blk, grad_att)
        return (normed.astype(jnp.bfloat16), grad_att, block_grad)
    output, grad_att, block_grad = lax.map(forward_block, (q_all, k_all, v_all, prefix_b, g_all))
    later = jnp.concatenate([jnp.cumsum(block_grad[::-1], axis=0)[::-1][1:], zero_state], axis=0)
    suffix_b = round_half(later)
    state_grad = lax.optimization_barrier(jnp.sum(block_grad, axis=0))

    def backward_block(items):
        q_blk, k_blk, v_blk, p_blk, s_blk, d_blk = items
        raw = jnp.einsum('thd,shd->hts', q_blk, k_blk)
        scores = round_half(jnp.where(causal[None], raw, 0.0))
        grad_scores = round_half(jnp.where(causal[None], jnp.einsum('the,she->hts', d_blk, v_blk), 0.0))
        q_grad = jnp.einsum('the,hde->thd', d_blk, p_blk) + jnp.einsum('hts,shd->thd', grad_scores, k_blk)
        k_grad = jnp.einsum('hts,thd->shd', grad_scores, q_blk) + jnp.einsum('she,hde->shd', v_blk, s_blk)
        v_grad = jnp.einsum('hts,the->she', scores, d_blk) + jnp.einsum('shd,hde->she', k_blk, s_blk)
        return (q_grad.astype(jnp.bfloat16), k_grad.astype(jnp.bfloat16), v_grad.astype(jnp.bfloat16))
    query_grad, key_grad, value_grad = lax.map(backward_block, (q_all, k_all, v_all, prefix_b, suffix_b, grad_att))
    flat = (blocks * TOK_DEV, HEADS * HEAD_DIM)
    return (output.reshape(flat), query_grad.reshape(flat), key_grad.reshape(flat), value_grad.reshape(flat), state_grad)
```

```python
import functools

import jax
import jax.numpy as jnp
from jax import lax
from jax.experimental import pallas as pl
from jax.experimental.pallas import tpu as pltpu
from jax.sharding import PartitionSpec as P

F32 = jnp.float32
BF16 = jnp.bfloat16
MESH = pl.DeviceIdType.MESH
CHUNK = 128


def nn(a, b):
    return lax.dot_general(a, b, (((1,), (0,)), ((), ())), preferred_element_type=F32)


def nt(a, b):
    return lax.dot_general(a, b, (((1,), (1,)), ((), ())), preferred_element_type=F32)


def tn(a, b):
    return lax.dot_general(a, b, (((0,), (0,)), ((), ())), preferred_element_type=F32)


def side(a, b):
    return jnp.concatenate([a, b], axis=1)


def stack(a, b):
    return jnp.concatenate([a, b], axis=0)


def diag(a, b):
    zero = jnp.zeros_like(a)
    return stack(side(a, zero), side(zero, b))


def rc(c):
    return pl.ds(c * CHUNK, CHUNK)


def rp(p):
    return pl.ds(2 * p * CHUNK, 2 * CHUNK)


def weave(*chains):
    slots = {}
    for chain in chains:
        for delay, steps in enumerate(chain):
            slots.setdefault(delay, []).append(steps)
    live, slot = [], 0
    while live or any(at >= slot for at in slots):
        live += slots.get(slot, [])
        live = [steps for steps in live if next(steps, "end") != "end"]
        slot += 1


def kernel(
    n, heads, dim, rows,
    q_hbm, k_hbm, v_hbm, i_hbm, g_hbm,
    out, dq, sg, k, v, acc_a, acc_b, after, gcum,
    q, g, init, score, da, cum, pre, state, grad,
    p1_in, p2_out, p2_in, p3_out, p3_in,
    b1_in, b2_out, b2_in, b3_out, t_out,
    sem_in, sem_init, one_send, one_recv, two_send, two_recv,
):
    gh = heads // 2
    chips = n // 2
    pairs = rows // (2 * CHUNK)
    step_heads = 2 - gh % 2
    me = lax.axis_index("ctx")
    core = lax.rem(me, 2)
    chip = me // 2
    partner = me + 1 - 2 * core
    peers = [2 * lax.rem(chip + j, chips) + core for j in range(1, chips)]
    mine = core * gh
    other = (1 - core) * gh

    barrier = pltpu.get_barrier_semaphore()
    for device in [partner] + peers:
        pl.semaphore_signal(barrier, inc=1, device_id={"ctx": device}, device_id_type=MESH)

    def strip(h):
        return pl.ds(pl.multiple_of(h * dim, dim), dim)

    def load(which, h):
        src, dst = ((k_hbm, k), (v_hbm, v), (q_hbm, q), (g_hbm, g))[which]
        return pltpu.make_async_copy(
            src.at[:, strip(h)], dst.at[h], sem_in.at[which, h]
        )

    load_init = pltpu.make_async_copy(i_hbm, init, sem_init)

    def issue(first, kinds):
        def step(i, _):
            h = lax.rem(first + i, heads)
            for kind in kinds:
                load(kind, h).start()
            return 0

        lax.fori_loop(0, heads, step, 0)

    issue(other, (0, 1))
    issue(mine, (2,))
    load_init.start()
    issue(mine, (3,))
    pl.semaphore_wait(barrier, chips)

    def to_partner(which, src, dst, i):
        return pltpu.make_async_remote_copy(
            src_ref=src, dst_ref=dst,
            send_sem=one_send.at[which, i], recv_sem=one_recv.at[which, i],
            device_id={"ctx": partner}, device_id_type=MESH,
        )

    def to_peer(which, j, src, dst, i):
        return pltpu.make_async_remote_copy(
            src_ref=src, dst_ref=dst,
            send_sem=two_send.at[which, j, i], recv_sem=two_recv.at[which, j, i],
            device_id={"ctx": peers[j]}, device_id_type=MESH,
        )

    def p1(i):
        return to_partner(0, state.at[other + i], p1_in.at[i], i)

    def p2(j, i):
        return to_peer(0, j, p2_out.at[i], p2_in.at[j, i], i)

    def p3(i):
        return to_partner(1, p3_out.at[i], p3_in.at[i], i)

    def b1(i):
        return to_partner(2, grad.at[mine + i], b1_in.at[i], i)

    def b2(j, i):
        return to_peer(1, j, b2_out.at[i], b2_in.at[j, i], i)

    def b3(i):
        return to_partner(3, b3_out.at[i], after.at[other + i], i)

    def bt(i):
        return to_partner(4, t_out.at[i], sg.at[other + i], i)

    def states(hs):
        for h in hs:
            load(0, h).wait()
            load(1, h).wait()
        turned = [[k[h, rp(p)].T for h in hs] for p in range(pairs)]
        parts = []
        for p in range(pairs):
            for h, across in zip(hs, turned[p]):
                a, b = v[h, rc(2 * p)], v[h, rc(2 * p + 1)]
                parts.append(nn(across, stack(side(a, a), side(jnp.zeros_like(b), b))))
        for s, h in enumerate(hs):
            total = jnp.zeros((dim, dim), F32)
            for p in range(pairs):
                part = parts[p * len(hs) + s]
                cum[h, 2 * p] = total
                cum[h, 2 * p + 1] = total + part[:, :dim]
                total = total + part[:, dim:]
            state[h] = total

    def states_other(i, _):
        states([other + i * step_heads + s for s in range(step_heads)])
        for s in range(step_heads):
            p1(i * step_heads + s).start()
        return 0

    lax.fori_loop(0, gh // step_heads, states_other, 0)

    def states_mine(i, _):
        states([mine + i * step_heads + s for s in range(step_heads)])
        for s in range(step_heads):
            t = i * step_heads + s
            p1(t).wait_recv()
            p2_out[t] = state[mine + t] + p1_in[t]
            for j in range(chips - 1):
                @pl.when(chip + j + 1 < chips)
                def _():
                    p2(j, t).start()
        return 0

    lax.fori_loop(0, gh // step_heads, states_mine, 0)

    causal = lax.broadcasted_iota(jnp.int32, (CHUNK, CHUNK), 0) >= lax.broadcasted_iota(
        jnp.int32, (CHUNK, CHUNK), 1
    )

    def masked(raw):
        return (
            jnp.where(causal, raw[:, :CHUNK], 0.0).astype(BF16),
            jnp.where(causal, raw[:, CHUNK:], 0.0).astype(BF16),
        )

    def within(i, _):
        hs = [lax.rem(mine + i * step_heads + s, heads) for s in range(step_heads)]
        for h in hs:
            load(2, h).wait()
        raws = []
        for h in hs:
            for p in range(pairs):
                a, b = (h, rc(2 * p)), (h, rc(2 * p + 1))
                raws.append((a, b, nt(side(q[a], q[b]), diag(k[a], k[b]))))
        for a, b, raw in raws:
            sa, sb = masked(raw)
            score[a] = sa
            score[b] = sb
        return 0

    lax.fori_loop(0, heads // step_heads, within, 0)
    load_init.wait()

    root = float(dim) ** 0.5

    def forward(h, prefix, p, parts):
        cs, ats = (2 * p, 2 * p + 1), ((h, rc(2 * p)), (h, rc(2 * p + 1)))
        xs = []
        for c, at in zip(cs, ats):
            pc = (prefix + cum[h, c]).astype(BF16)
            pre[h, c] = pc
            xs.append(nn(side(score[at], q[at]), stack(v[at], pc)))
        turned = q[h, rp(p)].T
        yield
        us, squares, along = [], [], []
        for x, at in zip(xs, ats):
            u = g[at].astype(F32)
            us.append(u)
            squares.append(jnp.sum(x * x, axis=-1, keepdims=True))
            along.append(jnp.sum(u * x, axis=-1, keepdims=True))
        yield
        das = []
        for x, u, sq, al, at in zip(xs, us, squares, along, ats):
            short = lax.rsqrt(sq + 1e-06 * dim)
            inv = root * short
            out[at] = (x * inv).astype(BF16)
            d = (u * inv - x * (short * short * inv * al)).astype(BF16)
            da[at] = d
            das.append(d)
        yield
        part = nn(
            turned,
            stack(side(das[0], jnp.zeros_like(das[0])), side(das[1], das[1])),
        )
        yield
        gcum[h, p] = part
        parts.append(part[:, :dim])

    def backward(h, p):
        a, b = (h, rc(2 * p)), (h, rc(2 * p + 1))
        da_a, da_b = da[a], da[b]
        raw = nt(side(da_a, da_b), diag(v[a], v[b]))
        turned = score[h, rp(p)].T
        yield
        sa, sb = masked(raw)
        grad_v = nn(turned, diag(da_a, da_b))
        turned = stack(sa, sb).T
        yield
        grad_q = nt(side(da_a, da_b), diag(pre[h, 2 * p], pre[h, 2 * p + 1])) + nn(
            side(sa, sb), diag(k[a], k[b])
        )
        acc_b[a] = grad_v[:, :dim]
        acc_b[b] = grad_v[:, dim:]
        yield
        grad_k = nn(turned, diag(q[a], q[b]))
        dq[a] = grad_q[:, :dim].astype(BF16)
        dq[b] = grad_q[:, dim:].astype(BF16)
        yield
        acc_a[a] = grad_k[:, :dim]
        acc_a[b] = grad_k[:, dim:]

    def both(h, prefix, before):
        load(3, h).wait()
        parts = []
        weave(
            [forward(h, prefix, p, parts) for p in range(pairs)],
            [backward(before, p) for p in range(pairs)],
        )
        grad[h] = functools.reduce(lambda x, y: x + y, parts)

    def heads_step(i, _):
        h = mine + i
        p3_out[i] = jnp.where(core == 0, state[h], 0.0)
        grad[h] = init[h] + jnp.where(core == 1, p1_in[i], 0.0)
        for j in range(chips - 1):
            @pl.when(chip >= j + 1)
            def _():
                p2(j, i).wait_recv()
                p3_out[i] = p3_out[i] + p2_in[j, i]
                grad[h] = grad[h] + p2_in[j, i]
        p3(i).start()
        both(h, grad[h], other + jnp.maximum(i - 1, 0))
        b1(i).start()
        p3(i).wait_recv()
        both(other + i, init[other + i] + p3_in[i], h)
        b1(i).wait_recv()
        b2_out[i] = grad[other + i] + b1_in[i]
        for j in range(chips - 1):
            b2(j, i).start()
        return 0

    lax.fori_loop(0, gh, heads_step, 0)
    weave([backward(other + gh - 1, p) for p in range(pairs)])

    def relay(i, _):
        h = other + i
        total = b2_out[i]
        later = jnp.zeros((dim, dim), F32)
        for j in range(chips - 1):
            b2(j, i).wait_recv()
            total = total + b2_in[j, i]
            later = later + jnp.where(chip >= j + 1, 0.0, b2_in[j, i])
        b3_out[i] = later + jnp.where(core == 1, grad[h], 0.0)
        b3(i).start()
        t_out[i] = total
        bt(i).start()
        sg[h] = total
        after[h] = later + jnp.where(core == 0, b1_in[i], 0.0)
        return 0

    lax.fori_loop(0, gh, relay, 0)

    def drain(i, _):
        b3(i).wait_recv()
        bt(i).wait_recv()
        p1(i).wait_send()
        p3(i).wait_send()
        b1(i).wait_send()
        b3(i).wait_send()
        bt(i).wait_send()
        for j in range(chips - 1):
            @pl.when(chip + j + 1 < chips)
            def _():
                p2(j, i).wait_send()
            b2(j, i).wait_send()
        return 0

    lax.fori_loop(0, gh, drain, 0)


def tail(
    heads, dim, rows,
    out, dq, sg, k, v, acc_a, acc_b, after, gcum,
    out_hbm, dq_hbm, dk_hbm, dv_hbm, sg_hbm,
    dk, dv, sem_whole, sem_head,
):
    pairs = rows // (2 * CHUNK)
    whole = pltpu.make_async_copy(sg, sg_hbm, sem_whole)

    def strip(h):
        return pl.ds(pl.multiple_of(h * dim, dim), dim)

    def store(which, h):
        src, dst = ((out, out_hbm), (dq, dq_hbm), (dk, dk_hbm), (dv, dv_hbm))[which]
        return pltpu.make_async_copy(
            src.at[h], dst.at[:, strip(h)], sem_head.at[which, h]
        )

    def first(h, _):
        store(0, h).start()
        store(1, h).start()
        return 0

    lax.fori_loop(0, heads, first, 0)
    whole.start()

    def finish(h, _):
        suffix = after[h]
        for p in reversed(range(pairs)):
            a, b = (h, rc(2 * p)), (h, rc(2 * p + 1))
            s_b = suffix.astype(BF16)
            s_a = (suffix + gcum[h, p, :, dim:]).astype(BF16)
            suffix = suffix + gcum[h, p, :, :dim]
            grad_k = nt(side(v[a], v[b]), diag(s_a, s_b))
            dk[a] = (acc_a[a] + grad_k[:, :dim]).astype(BF16)
            dk[b] = (acc_a[b] + grad_k[:, dim:]).astype(BF16)
            grad_v = nn(side(k[a], k[b]), diag(s_a, s_b))
            dv[a] = (acc_b[a] + grad_v[:, :dim]).astype(BF16)
            dv[b] = (acc_b[b] + grad_v[:, dim:]).astype(BF16)
        store(2, h).start()
        store(3, h).start()
        return 0

    lax.fori_loop(0, heads, finish, 0)

    def drain(h, _):
        for which in range(4):
            store(which, h).wait()
        return 0

    lax.fori_loop(0, heads, drain, 0)
    whole.wait()


def shards(n, queries, keys, values, init_state, out_grad):
    rows, width = queries.shape
    heads, dim, _ = init_state.shape
    gh = heads // 2
    chips = n // 2
    chunks = rows // CHUNK
    far = max(chips - 1, 1)
    flat = pltpu.VMEM((heads, rows, dim), BF16)
    wide = pltpu.VMEM((heads, rows, dim), F32)
    group = pltpu.VMEM((gh, dim, dim), F32)
    every = pltpu.VMEM((heads, dim, dim), F32)
    peers = pltpu.VMEM((far, gh, dim, dim), F32)
    dma = pltpu.SemaphoreType.DMA
    held = pl.pallas_call(
        functools.partial(kernel, n, heads, dim, rows),
        out_shape=[
            flat, flat, every, flat, flat, wide, wide, every,
            pltpu.VMEM((heads, chunks // 2, dim, 2 * dim), F32),
        ],
        in_specs=[pl.BlockSpec(memory_space=pltpu.HBM)] * 5,
        out_specs=[pl.BlockSpec(memory_space=pltpu.VMEM)] * 9,
        scratch_shapes=[
            flat, flat, every, flat, flat,
            pltpu.VMEM((heads, chunks, dim, dim), F32),
            pltpu.VMEM((heads, chunks, dim, dim), BF16),
            every, every,
            group, group, peers, group, group,
            group, group, peers, group, group,
            dma((4, heads)), dma,
            dma((5, gh)), dma((5, gh)),
            dma((2, far, gh)), dma((2, far, gh)),
        ],
        compiler_params=pltpu.CompilerParams(
            collective_id=0, has_side_effects=True, vmem_limit_bytes=32 * 1024 * 1024
        ),
    )(queries, keys, values, init_state, out_grad)
    flat_out = jax.ShapeDtypeStruct((rows, width), BF16)
    return pl.pallas_call(
        functools.partial(tail, heads, dim, rows),
        out_shape=[flat_out] * 4 + [jax.ShapeDtypeStruct((heads, dim, dim), F32)],
        in_specs=[pl.BlockSpec(memory_space=pltpu.VMEM)] * 9,
        out_specs=[pl.BlockSpec(memory_space=pl.ANY)] * 5,
        scratch_shapes=[flat, flat, dma, dma((4, heads))],
        compiler_params=pltpu.CompilerParams(vmem_limit_bytes=8 * 1024 * 1024),
    )(*held)


def solution(mesh):
    tokens = P(("grp", "ctx"), "head")
    states = P(("grp", "head"), None, None)
    return jax.shard_map(
        functools.partial(shards, mesh.shape["ctx"]),
        mesh=mesh,
        in_specs=(tokens, tokens, tokens, states, tokens),
        out_specs=(tokens, tokens, tokens, tokens, states),
        check_vma=False,
    )
```

```python
import functools

import jax
import jax.numpy as jnp
from jax import lax
from jax.experimental import pallas as pl
from jax.experimental.pallas import tpu as pltpu
from jax.sharding import PartitionSpec as P

F32 = jnp.float32
BF16 = jnp.bfloat16
MESH = pl.DeviceIdType.MESH
CHUNK = 128


def nn(a, b):
    return lax.dot_general(a, b, (((1,), (0,)), ((), ())), preferred_element_type=F32)


def nt(a, b):
    return lax.dot_general(a, b, (((1,), (1,)), ((), ())), preferred_element_type=F32)


def tn(a, b):
    return lax.dot_general(a, b, (((0,), (0,)), ((), ())), preferred_element_type=F32)


def side(a, b):
    return jnp.concatenate([a, b], axis=1)


def stack(a, b):
    return jnp.concatenate([a, b], axis=0)


def diag(a, b):
    zero = jnp.zeros_like(a)
    return stack(side(a, zero), side(zero, b))


def rc(c):
    return pl.ds(c * CHUNK, CHUNK)


def rp(p):
    return pl.ds(2 * p * CHUNK, 2 * CHUNK)


def weave(*chains):
    slots = {}
    for chain in chains:
        for delay, steps in enumerate(chain):
            slots.setdefault(delay, []).append(steps)
    live, slot = [], 0
    while live or any(at >= slot for at in slots):
        live += slots.get(slot, [])
        live = [steps for steps in live if next(steps, "end") != "end"]
        slot += 1


def kernel(
    n, heads, dim, rows,
    q_hbm, k_hbm, v_hbm, i_hbm, g_hbm,
    out, dq, sg, k, v, score, da, acc, after, gcum,
    q, g, init, cum, pre, state, grad,
    p1_in, p2_out, p2_in, p3_out, p3_in,
    b1_in, b2_out, b2_in, b3_out, t_out, ahead,
    sem_in, sem_init, one_send, one_recv, two_send, two_recv,
):
    gh = heads // 2
    chips = n // 2
    pairs = rows // (2 * CHUNK)
    step_heads = 4 if gh % 2 == 0 else 2
    me = lax.axis_index("ctx")
    core = lax.rem(me, 2)
    chip = me // 2
    partner = me + 1 - 2 * core
    peers = [2 * lax.rem(chip + j, chips) + core for j in range(1, chips)]
    mine = core * gh
    other = (1 - core) * gh

    barrier = pltpu.get_barrier_semaphore()
    for device in [partner] + peers:
        pl.semaphore_signal(barrier, inc=1, device_id={"ctx": device}, device_id_type=MESH)

    def strip(h):
        return pl.ds(pl.multiple_of(h * dim, dim), dim)

    def load(which, h):
        src, dst = ((k_hbm, k), (v_hbm, v), (q_hbm, q), (g_hbm, g))[which]
        return pltpu.make_async_copy(
            src.at[:, strip(h)], dst.at[h], sem_in.at[which, h]
        )

    load_init = pltpu.make_async_copy(i_hbm, init, sem_init)

    def issue(kinds):
        def step(i, _):
            for h in (other + i, mine + i):
                for kind in kinds:
                    load(kind, h).start()
            return 0

        lax.fori_loop(0, gh, step, 0)

    issue((0, 1))
    issue((2,))
    load_init.start()
    issue((3,))
    pl.semaphore_wait(barrier, chips)

    def to_partner(which, src, dst, i):
        return pltpu.make_async_remote_copy(
            src_ref=src, dst_ref=dst,
            send_sem=one_send.at[which, i], recv_sem=one_recv.at[which, i],
            device_id={"ctx": partner}, device_id_type=MESH,
        )

    def to_peer(which, j, src, dst, i):
        return pltpu.make_async_remote_copy(
            src_ref=src, dst_ref=dst,
            send_sem=two_send.at[which, j, i], recv_sem=two_recv.at[which, j, i],
            device_id={"ctx": peers[j]}, device_id_type=MESH,
        )

    def p1(i):
        return to_partner(0, state.at[other + i], p1_in.at[i], i)

    def p2(j, i):
        return to_peer(0, j, p2_out.at[i], p2_in.at[j, i], i)

    def p3(i):
        return to_partner(1, p3_out.at[i], p3_in.at[i], i)

    def b1(i):
        return to_partner(2, grad.at[mine + i], b1_in.at[i], i)

    def b2(j, i):
        return to_peer(1, j, b2_out.at[i], b2_in.at[j, i], i)

    def b3(i):
        return to_partner(3, b3_out.at[i], after.at[other + i], i)

    def bt(i):
        return to_partner(4, t_out.at[i], sg.at[other + i], i)

    def states(hs):
        for h in hs:
            load(0, h).wait()
            load(1, h).wait()
        turned = [[k[h, rp(p)].T for h in hs] for p in range(pairs)]
        parts = []
        for p in range(pairs):
            for h, across in zip(hs, turned[p]):
                a, b = v[h, rc(2 * p)], v[h, rc(2 * p + 1)]
                parts.append(nn(across, stack(side(a, a), side(jnp.zeros_like(b), b))))
        for s, h in enumerate(hs):
            total = jnp.zeros((dim, dim), F32)
            for p in range(pairs):
                part = parts[p * len(hs) + s]
                cum[h, 2 * p] = total
                cum[h, 2 * p + 1] = total + part[:, :dim]
                total = total + part[:, dim:]
            state[h] = total

    def send(i):
        p1(i).wait_recv()
        p2_out[i] = state[mine + i] + p1_in[i]
        for j in range(chips - 1):
            @pl.when(chip + j + 1 < chips)
            def _():
                p2(j, i).start()

    def states_step(i, _):
        states([other + i, mine + i])
        p1(i).start()

        @pl.when(i > 0)
        def _():
            send(i - 1)

        return 0

    lax.fori_loop(0, gh, states_step, 0)
    send(gh - 1)

    causal = lax.broadcasted_iota(jnp.int32, (CHUNK, CHUNK), 0) >= lax.broadcasted_iota(
        jnp.int32, (CHUNK, CHUNK), 1
    )

    def masked(raw):
        return (
            jnp.where(causal, raw[:, :CHUNK], 0.0).astype(BF16),
            jnp.where(causal, raw[:, CHUNK:], 0.0).astype(BF16),
        )

    def within(i, _):
        hs = [lax.rem(other + i * step_heads + s, heads) for s in range(step_heads)]
        for h in hs:
            load(2, h).wait()
        raws = []
        for h in hs:
            for p in range(pairs):
                a, b = (h, rc(2 * p)), (h, rc(2 * p + 1))
                raws.append((a, b, nt(side(q[a], q[b]), diag(k[a], k[b]))))
        for a, b, raw in raws:
            sa, sb = masked(raw)
            score[a] = sa
            score[b] = sb
        return 0

    lax.fori_loop(0, heads // step_heads, within, 0)
    load_init.wait()


    def forward(h, prefix, p, parts):
        cs, ats = (2 * p, 2 * p + 1), ((h, rc(2 * p)), (h, rc(2 * p + 1)))
        xs = []
        for c, at in zip(cs, ats):
            pc = (prefix + cum[h, c]).astype(BF16)
            pre[h, c] = pc
            xs.append(nn(side(score[at], q[at]), stack(v[at], pc)))
        turned = q[h, rp(p)].T
        yield
        us = [g[at].astype(F32) for at in ats]
        squares = [jnp.mean(x * x, axis=-1, keepdims=True) for x in xs]
        along = [jnp.mean(u * x, axis=-1, keepdims=True) for u, x in zip(us, xs)]
        yield
        das = []
        for x, u, sq, al, at in zip(xs, us, squares, along, ats):
            inv = lax.rsqrt(sq + 1e-06)
            normed = x * inv
            out[at] = normed.astype(BF16)
            d = (inv * (u - normed * (inv * al))).astype(BF16)
            da[at] = d
            das.append(d)
        yield
        part = nn(
            turned,
            stack(side(das[0], jnp.zeros_like(das[0])), side(das[1], das[1])),
        )
        yield
        gcum[h, p] = part
        parts.append(part[:, :dim])

    def backward(h, p):
        a, b = (h, rc(2 * p)), (h, rc(2 * p + 1))
        da_a, da_b = da[a], da[b]
        raw = nt(side(da_a, da_b), diag(v[a], v[b]))
        yield
        sa, sb = masked(raw)
        turned = stack(sa, sb).T
        grad_q = nt(side(da_a, da_b), diag(pre[h, 2 * p], pre[h, 2 * p + 1])) + nn(
            side(sa, sb), diag(k[a], k[b])
        )
        yield
        grad_k = nn(turned, diag(q[a], q[b]))
        dq[a] = grad_q[:, :dim].astype(BF16)
        dq[b] = grad_q[:, dim:].astype(BF16)
        yield
        acc[a] = grad_k[:, :dim]
        acc[b] = grad_k[:, dim:]

    def forward_of(work, *beside):
        sums = [[] for _ in work]
        weave(
            *[
                [forward(h, prefix, p, parts) for p in range(pairs)]
                for (h, prefix), parts in zip(work, sums)
            ],
            *beside,
        )
        for (h, _), parts in zip(work, sums):
            grad[h] = functools.reduce(lambda x, y: x + y, parts)

    def backward_of(h):
        return [backward(h, p) for p in range(pairs)]

    def pass_on(i):
        b1(i).wait_recv()
        b2_out[i] = grad[other + i] + b1_in[i]
        for j in range(chips - 1):
            b2(j, i).start()

    def heads_step(i, _):
        h = mine + i
        p3_out[i] = jnp.where(core == 0, state[h], 0.0)
        ahead[0] = init[h] + jnp.where(core == 1, p1_in[i], 0.0)
        for j in range(chips - 1):
            @pl.when(chip >= j + 1)
            def _():
                p2(j, i).wait_recv()
                p3_out[i] = p3_out[i] + p2_in[j, i]
                ahead[0] = ahead[0] + p2_in[j, i]
        p3(i).start()

        last = jnp.maximum(i - 1, 0)

        @pl.when(i > 0)
        def _():
            p3(i - 1).wait_recv()
            ahead[1] = init[other + i - 1] + p3_in[i - 1]

        load(3, h).wait()

        @pl.when(i > 1)
        def _():
            load(3, other + i - 1).wait()

        back = other + last
        forward_of([(h, ahead[0]), (back, ahead[1])])
        b1(i).start()

        @pl.when(i > 0)
        def _():
            pass_on(i - 1)

        return 0

    load(3, other).wait()
    ahead[1] = init[other]
    lax.fori_loop(0, gh, heads_step, 0)
    final = other + gh - 1
    if gh > 1:
        load(3, final).wait()
    p3(gh - 1).wait_recv()
    forward_of([(final, init[final] + p3_in[gh - 1])])
    pass_on(gh - 1)

    def rest(i, _):
        weave(backward_of(mine + i), backward_of(other + i))
        return 0

    lax.fori_loop(0, gh - 1, rest, 0)

    def relay(i, _):
        h = other + i
        total = b2_out[i]
        later = jnp.zeros((dim, dim), F32)
        for j in range(chips - 1):
            b2(j, i).wait_recv()
            total = total + b2_in[j, i]
            later = later + jnp.where(chip >= j + 1, 0.0, b2_in[j, i])
        b3_out[i] = later + jnp.where(core == 1, grad[h], 0.0)
        b3(i).start()
        t_out[i] = total
        bt(i).start()
        sg[h] = total
        after[h] = later + jnp.where(core == 0, b1_in[i], 0.0)
        return 0

    lax.fori_loop(0, gh, relay, 0)
    lax.fori_loop(gh - 1, gh, rest, 0)

    def drain(i, _):
        b3(i).wait_recv()
        bt(i).wait_recv()
        p1(i).wait_send()
        p3(i).wait_send()
        b1(i).wait_send()
        b3(i).wait_send()
        bt(i).wait_send()
        for j in range(chips - 1):
            @pl.when(chip + j + 1 < chips)
            def _():
                p2(j, i).wait_send()
            b2(j, i).wait_send()
        return 0

    lax.fori_loop(0, gh, drain, 0)


def tail(
    heads, dim, rows,
    out, dq, sg, k, v, score, da, acc, after, gcum,
    out_hbm, dq_hbm, dk_hbm, dv_hbm, sg_hbm,
    dk, dv, sem_whole, sem_head,
):
    pairs = rows // (2 * CHUNK)
    whole = pltpu.make_async_copy(sg, sg_hbm, sem_whole)

    def strip(h):
        return pl.ds(pl.multiple_of(h * dim, dim), dim)

    def store(which, h):
        src, dst = ((out, out_hbm), (dq, dq_hbm), (dk, dk_hbm), (dv, dv_hbm))[which]
        return pltpu.make_async_copy(
            src.at[h], dst.at[:, strip(h)], sem_head.at[which, h]
        )

    def first(h, _):
        store(0, h).start()
        store(1, h).start()
        return 0

    lax.fori_loop(0, heads, first, 0)
    whole.start()

    def finish(h):
        suffix = after[h]
        cuts = []
        for p in reversed(range(pairs)):
            s_b = suffix.astype(BF16)
            s_a = (suffix + gcum[h, p, :, dim:]).astype(BF16)
            suffix = suffix + gcum[h, p, :, :dim]
            cuts.append((s_a, s_b))

        def pair(p, s_a, s_b):
            a, b = (h, rc(2 * p)), (h, rc(2 * p + 1))
            turned = score[h, rp(p)].T
            ends = diag(s_a, s_b)
            grad_k = nt(side(v[a], v[b]), ends)
            yield
            grad_v = nn(turned, diag(da[a], da[b])) + nn(side(k[a], k[b]), ends)
            dk[a] = (acc[a] + grad_k[:, :dim]).astype(BF16)
            dk[b] = (acc[b] + grad_k[:, dim:]).astype(BF16)
            yield
            dv[a] = grad_v[:, :dim].astype(BF16)
            dv[b] = grad_v[:, dim:].astype(BF16)

        return [pair(p, *cut) for p, cut in zip(reversed(range(pairs)), cuts)]

    def finish_two(i, _):
        weave(finish(2 * i), finish(2 * i + 1))
        for h in (2 * i, 2 * i + 1):
            store(2, h).start()
            store(3, h).start()
        return 0

    lax.fori_loop(0, heads // 2, finish_two, 0)

    def drain(h, _):
        for which in range(4):
            store(which, h).wait()
        return 0

    lax.fori_loop(0, heads, drain, 0)
    whole.wait()


def shards(n, queries, keys, values, init_state, out_grad):
    rows, width = queries.shape
    heads, dim, _ = init_state.shape
    gh = heads // 2
    chips = n // 2
    chunks = rows // CHUNK
    far = max(chips - 1, 1)
    flat = pltpu.VMEM((heads, rows, dim), BF16)
    group = pltpu.VMEM((gh, dim, dim), F32)
    every = pltpu.VMEM((heads, dim, dim), F32)
    peers = pltpu.VMEM((far, gh, dim, dim), F32)
    dma = pltpu.SemaphoreType.DMA
    held = pl.pallas_call(
        functools.partial(kernel, n, heads, dim, rows),
        out_shape=[
            flat, flat, every, flat, flat, flat, flat,
            pltpu.VMEM((heads, rows, dim), F32), every,
            pltpu.VMEM((heads, chunks // 2, dim, 2 * dim), F32),
        ],
        in_specs=[pl.BlockSpec(memory_space=pltpu.HBM)] * 5,
        out_specs=[pl.BlockSpec(memory_space=pltpu.VMEM)] * 10,
        scratch_shapes=[
            flat, flat, every,
            pltpu.VMEM((heads, chunks, dim, dim), F32),
            pltpu.VMEM((heads, chunks, dim, dim), BF16),
            every, every,
            group, group, peers, group, group,
            group, group, peers, group, group,
            pltpu.VMEM((2, dim, dim), F32),
            dma((4, heads)), dma,
            dma((5, gh)), dma((5, gh)),
            dma((2, far, gh)), dma((2, far, gh)),
        ],
        compiler_params=pltpu.CompilerParams(
            collective_id=0, has_side_effects=True, vmem_limit_bytes=40 * 1024 * 1024
        ),
    )(queries, keys, values, init_state, out_grad)
    flat_out = jax.ShapeDtypeStruct((rows, width), BF16)
    return pl.pallas_call(
        functools.partial(tail, heads, dim, rows),
        out_shape=[flat_out] * 4 + [jax.ShapeDtypeStruct((heads, dim, dim), F32)],
        in_specs=[pl.BlockSpec(memory_space=pltpu.VMEM)] * 10,
        out_specs=[pl.BlockSpec(memory_space=pl.ANY)] * 5,
        scratch_shapes=[flat, flat, dma, dma((4, heads))],
        compiler_params=pltpu.CompilerParams(vmem_limit_bytes=8 * 1024 * 1024),
    )(*held)


def solution(mesh):
    tokens = P(("grp", "ctx"), "head")
    states = P(("grp", "head"), None, None)
    return jax.shard_map(
        functools.partial(shards, mesh.shape["ctx"]),
        mesh=mesh,
        in_specs=(tokens, tokens, tokens, states, tokens),
        out_specs=(tokens, tokens, tokens, tokens, states),
        check_vma=False,
    )
```
